256 devices in a mesh: gx: 4 (over y), gy: 16 (over z, core), sa: 4 (over x).
Axes of the slice: x: 4, y: 4, z: 8, core: 2. Of those that a mesh axis runs over, the one named last changes fastest.
Arguments:
- tokens: bfloat16 [192, 4, 8192], P(None, None, 'gx'), may hold values from -6 to 6
- norm_gain: bfloat16 [8192], P('gx'), may hold values from 0.099609375 to 1.8984375
- w_query: bfloat16 [8192, 8192], P('gx', 'gy'), may hold values from -0.125 to 0.125
- w_keyval: bfloat16 [8192, 2048], P('gx', 'gy'), may hold values from -0.0625 to 0.0625
- w_out: bfloat16 [8192, 8192], P('gy', 'gx'), may hold values from -0.09375 to 0.09375
- paged_key_cache: bfloat16 [2048, 128, 1024], P(('gx', 'gy', 'sa')), may hold values from -256 to 256
- paged_value_cache: bfloat16 [2048, 128, 1024], P(('gx', 'gy', 'sa')), may hold values from -12 to 12
- lengths: int32 [192], replicated, may hold values from 1 to 8192, as said below
- slot_owner: int32 [2048], P(('gx', 'gy', 'sa')), may hold values from 0 to 191, as said below
- slot_page_number: int32 [2048], P(('gx', 'gy', 'sa')), may hold values from -1 to 63, as said below
Outputs:
- mixed: float32 [192, 4, 8192], P(None, None, ('gx', 'gy'))
- appended_key_value: bfloat16 [192, 4, 2048], P('gx', None, 'gy')
The draws below stay inside these ranges and needn't reach their ends.
Inputs may be any that keep to these rules, and one draw needn't show every extreme that they name: `lengths`: in each group of 48 consecutive requests, 4 hold 4096 to 8192 positions, one of them exactly 8192, and the others 1 to 512, one of them exactly 512. Slot s belongs to group s // 512, and its owner is a request of that group (slot_owner[s] // 48 == s // 512). Every page p < ceil(lengths[r] / 128) of request r is held by exactly one slot; a slot that holds no page has slot_page_number -1 and the group's first request as owner. `slot_page_number`: laid out with slot_owner as stated there.
All inputs are finite; a program needn't handle non-finite values.
Results may differ from the reference program's by a relative error of at most 0.005.
The reference program's roundings to bfloat16 on the way count: a program that leaves them out, or rounds other values in their place, can miss the bound.
Values may be sent and summed in bfloat16 or wider, within the bound.
A program may use at most 128 MiB of HBM per device.

```python
import jax
import jax.numpy as jnp
from jax import lax

D = 8192
QUERY_HEADS = 64
KEY_VALUE_HEADS = 8
HEAD_ENTRIES = 128
QW = 8192
KVW = 2048
DECODE_STEPS = 4
PAGE_POSITIONS = 128
SHORT_LEN = 512
LOCAL_SLOTS = 512
TOTAL_SLOTS = 2048
REQUEST_GROUP = 48
REQUEST_COUNT = 192
LONG_GRP = 4
LONG_LEN = 8192
N_GX = 4


def shuffled(subkey, groups, length):

    def one_order(item_key):
        return jax.random.permutation(item_key, length)
    return jax.vmap(one_order)(jax.random.split(subkey, groups)).astype(jnp.int32)


def request_layout(key):
    groups = REQUEST_COUNT // REQUEST_GROUP
    order = shuffled(jax.random.fold_in(key, 31), groups, REQUEST_GROUP)
    ranking = jnp.argsort(order, axis=1).astype(jnp.int32)
    long_draw = jax.random.randint(jax.random.fold_in(key, 32), (groups, REQUEST_GROUP), LONG_LEN // 2, LONG_LEN + 1)
    short_draw = jax.random.randint(jax.random.fold_in(key, 33), (groups, REQUEST_GROUP), 1, SHORT_LEN + 1)
    long_value = jnp.where(ranking == 0, LONG_LEN, long_draw)
    short_value = jnp.where(ranking == LONG_GRP, SHORT_LEN, short_draw)
    request_lengths = jnp.where(ranking < LONG_GRP, long_value, short_value).astype(jnp.int32)
    page_counts = (request_lengths + PAGE_POSITIONS - 1) // PAGE_POSITIONS
    page_ends = jnp.cumsum(page_counts, axis=1)
    page_starts = page_ends - page_counts
    slot_rank = jnp.arange(LOCAL_SLOTS, dtype=jnp.int32)
    which_request = jnp.sum((page_ends[:, None, :] <= slot_rank[None, :, None]).astype(jnp.int32), axis=2)
    used_slot = which_request < REQUEST_GROUP
    safe_request = jnp.minimum(which_request, REQUEST_GROUP - 1)
    page_number = slot_rank[None, :] - jnp.take_along_axis(page_starts, safe_request, axis=1)
    group_base = jnp.arange(groups, dtype=jnp.int32)[:, None] * REQUEST_GROUP
    owner_rank = jnp.where(used_slot, group_base + safe_request, group_base)
    page_rank = jnp.where(used_slot, page_number, -1)
    placing = shuffled(jax.random.fold_in(key, 34), groups, LOCAL_SLOTS)
    inverse = jnp.argsort(placing, axis=1).astype(jnp.int32)
    owners = jnp.take_along_axis(owner_rank, inverse, axis=1)
    pages = jnp.take_along_axis(page_rank, inverse, axis=1)
    return (request_lengths.reshape(-1).astype(jnp.int32), owners.reshape(-1).astype(jnp.int32), pages.reshape(-1).astype(jnp.int32))


def draw_lengths(key, part):
    return request_layout(key)[0]


def draw_slot_owner(key, part):
    return request_layout(key)[1]


def draw_slot_page_number(key, part):
    return request_layout(key)[2]


def draw_paged_key_cache(key, part):
    array_shape = (TOTAL_SLOTS, PAGE_POSITIONS, KEY_VALUE_HEADS * HEAD_ENTRIES)
    values = jnp.clip(jax.random.normal(jax.random.fold_in(key, 45), array_shape, jnp.float32), -4.0, 4.0)
    return values.astype(jnp.bfloat16)


def with_spikes(entries, own_key, source, target, parts, factor):
    owner, partner = [(jnp.arange(entries.shape[axis_at]) // (entries.shape[axis_at] // parts)).reshape([-1 if axis == axis_at else 1 for axis in range(entries.ndim)]) for axis_at in (source, target)]
    chosen = jax.random.permutation(own_key, parts)[partner]
    strong = (owner == chosen) | (owner == (partner + parts // 2) % parts)
    return jnp.where(strong, factor * entries, entries)


def block_scale(stream_key, shape, cuts, low, top_value):
    level = 1.0
    for axis_at, parts in cuts:
        heights = jax.random.uniform(jax.random.fold_in(jax.random.fold_in(stream_key, 6), axis_at), (parts,), jnp.float32, low / len(cuts), top_value / len(cuts))
        level = level * jnp.repeat(jnp.exp(heights), shape[axis_at] // parts).reshape((-1,) + (1,) * (len(shape) - 1 - axis_at))
    return level


def centred(stream_key, extent, width, most, pieces=(), kind=jnp.bfloat16):
    factor_of = block_scale(stream_key, extent, pieces, -0.22, 0.18) if pieces else 1.0
    values = jax.random.normal(stream_key, extent, jnp.float32) * width * factor_of
    return jnp.minimum(jnp.maximum(values, -most), most).astype(kind)


def bell_draw_with(rng, shape, scale, reach, pieces, heavy, held_as=jnp.bfloat16):
    drawn = scale * jax.random.normal(rng, shape, jnp.float32)
    if pieces:
        drawn = drawn * block_scale(rng, shape, pieces, -0.22, 0.18)
    return jnp.clip(with_spikes(drawn, jax.random.fold_in(rng, 3), *heavy), -reach, reach).astype(held_as)


def setup_inputs(seed: int = 0) -> dict:
    streams_of = jax.random.split(jax.random.key(seed), 11)
    return {
        "tokens": centred(streams_of[0], (REQUEST_COUNT, DECODE_STEPS, D), 1.0, 6.0, ((2, 4),)),
        "norm_gain": jnp.clip(1.0 + 0.18 * jax.random.normal(streams_of[1], (D,), jnp.float32), 0.099609375, 1.8984375).astype(jnp.bfloat16),
        "w_query": centred(streams_of[2], (D, QW), (D // 4) ** -0.5, 0.125, ((0, 4), (1, 16))),
        "w_keyval": centred(streams_of[3], (D, KVW), D ** -0.5, 0.0625, ((0, 4), (1, 16))),
        "w_out": bell_draw_with(streams_of[4], (QW, D), QW ** -0.5, 0.09375, ((0, 16), (1, 4)), (0, 1, 16, 2.0)),
        "paged_key_cache": draw_paged_key_cache(jax.random.fold_in(streams_of[10], 71), 0),
        "paged_value_cache": centred(streams_of[6], (TOTAL_SLOTS, PAGE_POSITIONS, KEY_VALUE_HEADS * HEAD_ENTRIES), 2.0, 12.0, ((0, 256),)),
        "lengths": draw_lengths(jax.random.fold_in(streams_of[10], 71), 0),
        "slot_owner": draw_slot_owner(jax.random.fold_in(streams_of[10], 71), 0),
        "slot_page_number": draw_slot_page_number(jax.random.fold_in(streams_of[10], 71), 0),
    }


rope_base = 500000.0
norm_eps = 1e-05
neg_fill = -1e+30
precise = lax.Precision.HIGHEST

def apply_rotary(head_rows, token_positions):
    half_dim = head_rows.shape[-1] // 2
    exponent = jnp.arange(half_dim, dtype=jnp.float32) * (-2.0 / head_rows.shape[-1])
    inverse_freq = jnp.power(jnp.float32(rope_base), exponent)
    angles = token_positions.astype(jnp.float32)[..., None, None] * inverse_freq
    cosine = jnp.cos(angles)
    sine_value = jnp.sin(angles)
    front_half = head_rows[..., :half_dim]
    back_half = head_rows[..., half_dim:]
    return jnp.concatenate([front_half * cosine - back_half * sine_value, back_half * cosine + front_half * sine_value], axis=-1)

def group_attention(packed_rows):
    rotated_query, key_new, fresh_value, key_page_blocks, value_page_blocks, group_lengths, local_request_owner, page_index = packed_rows
    slot_ordinal = key_page_blocks.shape[0]
    heads_per_group = QUERY_HEADS // KEY_VALUE_HEADS
    score_scale = HEAD_ENTRIES ** (-0.5)
    member_mask = local_request_owner[None, :] == jnp.arange(REQUEST_GROUP, dtype=jnp.int32)[:, None]
    member = member_mask.astype(jnp.float32)
    slot_length = jnp.take(group_lengths, local_request_owner)
    cache_positions = page_index[:, None] * PAGE_POSITIONS + jnp.arange(PAGE_POSITIONS, dtype=jnp.int32)[None, :]
    live_slots = (page_index[:, None] >= 0) & (cache_positions < slot_length[:, None])
    live_mask = live_slots[:, None, None, None, :]
    slot_queries = jnp.take(rotated_query, local_request_owner, axis=0).astype(jnp.float32).reshape(slot_ordinal, DECODE_STEPS, KEY_VALUE_HEADS, heads_per_group, HEAD_ENTRIES)
    widened_keys = key_page_blocks.astype(jnp.float32).reshape(slot_ordinal, PAGE_POSITIONS, KEY_VALUE_HEADS, HEAD_ENTRIES)
    widened_values = value_page_blocks.astype(jnp.float32).reshape(slot_ordinal, PAGE_POSITIONS, KEY_VALUE_HEADS, HEAD_ENTRIES)
    scores = jnp.einsum('suhgd,sphd->suhgp', slot_queries, widened_keys, precision=precise) * score_scale
    scores = jnp.where(live_mask, scores, neg_fill)
    slot_top = lax.optimization_barrier(jnp.max(scores, axis=-1))
    cache_top = lax.optimization_barrier(jnp.max(jnp.where(member_mask[:, :, None, None, None], slot_top[None], neg_fill), axis=1))
    request_queries = rotated_query.astype(jnp.float32).reshape(REQUEST_GROUP, DECODE_STEPS, KEY_VALUE_HEADS, heads_per_group, HEAD_ENTRIES)
    fresh_scores = jnp.einsum('ruhgd,rvhd->ruhgv', request_queries, key_new.astype(jnp.float32), precision=precise) * score_scale
    seen_mask = (jnp.arange(DECODE_STEPS, dtype=jnp.int32)[:, None] >= jnp.arange(DECODE_STEPS, dtype=jnp.int32)[None, :])[None, :, None, None, :]
    fresh_scores = jnp.where(seen_mask, fresh_scores, neg_fill)
    top_score = jnp.maximum(cache_top, lax.optimization_barrier(jnp.max(fresh_scores, axis=-1)))
    slot_tops = jnp.take(top_score, local_request_owner, axis=0)
    weights = jnp.where(live_mask, jnp.exp(scores - slot_tops[..., None]), 0.0)
    fresh_weights = jnp.where(seen_mask, jnp.exp(fresh_scores - top_score[..., None]), 0.0)
    denominator = jnp.einsum('rs,suhg->ruhg', member, lax.optimization_barrier(jnp.sum(weights, axis=-1)), precision=precise) + lax.optimization_barrier(jnp.sum(fresh_weights, axis=-1))
    rounded = lax.optimization_barrier(weights.astype(jnp.bfloat16)).astype(jnp.float32)
    rounded_fresh = lax.optimization_barrier(fresh_weights.astype(jnp.bfloat16)).astype(jnp.float32)
    slot_values = jnp.einsum('suhgp,sphd->suhgd', rounded, widened_values, precision=precise)
    numerator = jnp.einsum('rs,suhgd->ruhgd', member, slot_values, precision=precise)
    numerator = numerator + jnp.einsum('ruhgv,rvhd->ruhgd', rounded_fresh, fresh_value.astype(jnp.float32), precision=precise)
    attended = (numerator / denominator[..., None]).astype(jnp.bfloat16)
    return attended.reshape(REQUEST_GROUP, DECODE_STEPS, QUERY_HEADS * HEAD_ENTRIES)

def reference(tokens, norm_gain, w_query, w_keyval, w_out, paged_key_cache, paged_value_cache, lengths, slot_owner, slot_page_number):
    as_float = tokens.astype(jnp.float32)
    mean_square = lax.optimization_barrier(jnp.mean(as_float * as_float, axis=-1))
    normed = (as_float * lax.rsqrt(mean_square + norm_eps)[..., None] * norm_gain.astype(jnp.float32)).astype(jnp.bfloat16)
    flat_rows = normed.reshape(REQUEST_COUNT * DECODE_STEPS, D)
    query = jnp.dot(flat_rows, w_query, preferred_element_type=jnp.float32).astype(jnp.bfloat16)
    key_value_pair = jnp.dot(flat_rows, w_keyval, preferred_element_type=jnp.float32).astype(jnp.bfloat16).reshape(REQUEST_COUNT, DECODE_STEPS, KVW)
    token_positions = lengths[:, None] + jnp.arange(DECODE_STEPS, dtype=jnp.int32)[None, :]
    rotated_query = apply_rotary(query.astype(jnp.float32).reshape(REQUEST_COUNT, DECODE_STEPS, QUERY_HEADS, HEAD_ENTRIES), token_positions).astype(jnp.bfloat16)
    rotated_key = apply_rotary(key_value_pair[..., :KEY_VALUE_HEADS * HEAD_ENTRIES].astype(jnp.float32).reshape(REQUEST_COUNT, DECODE_STEPS, KEY_VALUE_HEADS, HEAD_ENTRIES), token_positions).astype(jnp.bfloat16)
    fresh_value = key_value_pair[..., KEY_VALUE_HEADS * HEAD_ENTRIES:].reshape(REQUEST_COUNT, DECODE_STEPS, KEY_VALUE_HEADS, HEAD_ENTRIES)
    appended_key_value = jnp.concatenate([rotated_key.reshape(REQUEST_COUNT, DECODE_STEPS, KEY_VALUE_HEADS * HEAD_ENTRIES), key_value_pair[..., KEY_VALUE_HEADS * HEAD_ENTRIES:]], axis=-1)
    local_request_owner = slot_owner.reshape(N_GX, LOCAL_SLOTS) - jnp.arange(N_GX, dtype=jnp.int32)[:, None] * REQUEST_GROUP
    packed_rows = (rotated_query.reshape(N_GX, REQUEST_GROUP, DECODE_STEPS, QUERY_HEADS, HEAD_ENTRIES), rotated_key.reshape(N_GX, REQUEST_GROUP, DECODE_STEPS, KEY_VALUE_HEADS, HEAD_ENTRIES), fresh_value.reshape(N_GX, REQUEST_GROUP, DECODE_STEPS, KEY_VALUE_HEADS, HEAD_ENTRIES), paged_key_cache.reshape(N_GX, LOCAL_SLOTS, PAGE_POSITIONS, KEY_VALUE_HEADS * HEAD_ENTRIES), paged_value_cache.reshape(N_GX, LOCAL_SLOTS, PAGE_POSITIONS, KEY_VALUE_HEADS * HEAD_ENTRIES), lengths.reshape(N_GX, REQUEST_GROUP), local_request_owner, slot_page_number.reshape(N_GX, LOCAL_SLOTS))
    attended = lax.map(group_attention, packed_rows).reshape(REQUEST_COUNT * DECODE_STEPS, QW)
    mixed = jnp.dot(attended, w_out, preferred_element_type=jnp.float32).reshape(REQUEST_COUNT, DECODE_STEPS, D)
    return (mixed, appended_key_value)
```

```python
import jax
import jax.numpy as jnp
from jax import lax
from jax.experimental import pallas as pl
from jax.experimental.pallas import tpu as pltpu
from jax.sharding import PartitionSpec as P

D = 8192
QUERY_HEADS = 64
KEY_VALUE_HEADS = 8
HEAD = 128
GROUPS = 4
MEMBERS = 48
STEPS = 4
SLOTS = 8
PAGE = 128
PEERS = 64
ZN = 8
ROWS = GROUPS * MEMBERS

rope_base = 500000.0
norm_eps = 1e-05
neg_fill = -1e30
MESH = pl.DeviceIdType.MESH
f32 = jnp.float32
bf16 = jnp.bfloat16


def dot(a, b):
    return jnp.dot(a, b, preferred_element_type=f32)


def dot_nt(a, b):
    return lax.dot_general(a, b, (((1,), (1,)), ((), ())), preferred_element_type=f32)


def iota(shape, axis):
    return lax.broadcasted_iota(jnp.int32, shape, axis)


def lanes(index):
    return pl.ds(pl.multiple_of(index * HEAD, HEAD), HEAD)


def z_offset(k):
    return jnp.where(lax.rem(k, 2) == 1, (k + 1) // 2, lax.rem(ZN - k // 2, ZN))


def drain(ref, sem):
    pltpu.make_async_copy(ref, ref, sem).wait()


def kernel(
    x_ref, gain_ref, cos_ref, sin_ref, len_ref, own_ref, page_ref,
    wq_hbm, wkv_hbm, wo_hbm, k_hbm, v_hbm,
    out_ref, app_ref,
    wq, wkv, wo, kb, vb, xn, sqcol, sqs, ohs, ohr, live, perm, permt,
    qps, qpr, kps, kpr, qp, qsend, qrecv, kvs, appr, nkv, osend, orecv,
    lsend, lrecv, asend, arecv, acc, psend, precv, zsend, zrecv,
    load_sem, sq_s, sq_r, oh_s, oh_r, qp_s, qp_r, kp_s, kp_r, q_s, q_r,
    app_s, app_r, nk_s, nk_r, o_s, o_r, l_s, l_r, a_s, a_r,
    p_s, p_r, z_s, z_r, x_s, x_r,
):
    gx = lax.axis_index("gx")
    gy = lax.axis_index("gy")
    sa = lax.axis_index("sa")
    z = gy // 2
    core = lax.rem(gy, 2)
    me = gy * 4 + sa

    def remote(src, dst, ss, rs, dev):
        return pltpu.make_async_remote_copy(
            src_ref=src, dst_ref=dst, send_sem=ss, recv_sem=rs,
            device_id=dev, device_id_type=MESH,
        )

    loads = [
        pltpu.make_async_copy(a, b, load_sem.at[i])
        for i, (a, b) in enumerate(
            [(wq_hbm, wq), (wkv_hbm, wkv), (k_hbm, kb), (v_hbm, vb), (wo_hbm, wo)]
        )
    ]
    for c in loads:
        c.start()

    barrier = pltpu.get_barrier_semaphore()

    def greet(k, carry):
        peer = lax.rem(me + k, PEERS)
        pl.semaphore_signal(
            barrier, inc=1, device_id=(gx, peer // 4, lax.rem(peer, 4)), device_id_type=MESH
        )
        return carry

    lax.fori_loop(1, PEERS, greet, 0)

    def greet_y(k, carry):
        pl.semaphore_signal(
            barrier, inc=1,
            device_id=(lax.rem(gx + 1 + k // 4, GROUPS), gy, lax.rem(k, 4)),
            device_id_type=MESH,
        )
        return carry

    lax.fori_loop(0, 12, greet_y, 0)

    def square(i, carry):
        rows = pl.ds(pl.multiple_of(i * 16, 16), 16)
        xf = x_ref[rows, :].astype(f32)
        s = jnp.sum(xf * xf, axis=1, keepdims=True)
        sqcol[rows, :] = jnp.broadcast_to(s, (16, 128))
        return carry

    lax.fori_loop(0, ROWS // 16, square, 0)
    row128 = iota((128, 128), 0)
    lane128 = iota((128, 128), 1)
    eye = row128 == lane128
    r0 = jnp.sum(jnp.where(eye, sqcol[0:128, :], 0.0), axis=0, keepdims=True)
    r1 = jnp.sum(jnp.where(eye[0:64, :], sqcol[128:192, :], 0.0), axis=0, keepdims=True)
    sqs[gx, :, 0:128] = r0
    sqs[gx, :, 128:256] = r1

    row8 = iota((SLOTS, 128), 0)
    lane8 = iota((SLOTS, 128), 1)
    owner = jnp.zeros((SLOTS, 128), jnp.int32)
    for s in range(SLOTS):
        who = own_ref[s]
        page = page_ref[s]
        left = jnp.where(page >= 0, len_ref[who] - page * PAGE, 0)
        live[pl.ds(32 * s, 32), :] = (iota((32, 128), 1) < left).astype(f32)
        owner = jnp.where(row8 == s, who - gx * MEMBERS, owner)
    onehot = (lane8 == owner).astype(f32).astype(bf16)
    ohs[...] = onehot
    ohr[me] = onehot

    pl.semaphore_wait(barrier, PEERS - 1 + 12)

    for k in range(1, GROUPS):
        remote(
            sqs.at[gx], sqs.at[gx], sq_s.at[k - 1], sq_r.at[gx],
            (lax.rem(gx + k, GROUPS), gy, sa),
        ).start()

    def send_owner(k, carry):
        peer = lax.rem(me + k, PEERS)
        remote(ohs, ohr.at[me], oh_s, oh_r, (gx, peer // 4, lax.rem(peer, 4))).start()
        return carry

    lax.fori_loop(1, PEERS, send_owner, 0)

    pr = iota((256, 256), 0)
    pc = iota((256, 256), 1)
    want = ((pr >> 3) & 3) * 64 + (pr & 7) * 8 + (pr >> 5)
    perm[...] = (pc == want).astype(f32).astype(bf16)
    want = (pr & 7) * 32 + (pr >> 6) * 8 + ((pr >> 3) & 7)
    permt[...] = (pc == want).astype(f32).astype(bf16)
    qp[...] = jnp.zeros_like(qp)

    for k in range(1, GROUPS):
        src = lax.rem(gx + k, GROUPS)
        drain(sqs.at[src], sq_r.at[src])
    total = sqs[0] + sqs[1] + sqs[2] + sqs[3]
    t0 = jnp.broadcast_to(total[:, 0:128], (128, 128))
    t1 = jnp.broadcast_to(total[:, 128:256], (64, 128))
    c0 = jnp.sum(jnp.where(eye, t0, 0.0), axis=1, keepdims=True)
    c1 = jnp.sum(jnp.where(eye[0:64, :], t1, 0.0), axis=1, keepdims=True)
    sqcol[0:128, :] = jnp.broadcast_to(lax.rsqrt(c0 / D + norm_eps), (128, 128))
    sqcol[128:192, :] = jnp.broadcast_to(lax.rsqrt(c1 / D + norm_eps), (64, 128))

    def normalise(i, carry):
        rows = pl.ds(pl.multiple_of(i * 16, 16), 16)
        inv = sqcol[rows, 0:1]
        xf = x_ref[rows, :].astype(f32)
        xn[rows, :] = (xf * inv * gain_ref[...].astype(f32)).astype(bf16)
        return carry

    lax.fori_loop(0, ROWS // 16, normalise, 0)

    loads[0].wait()
    for n in range(2):
        part = dot(xn[...], wq[:, 256 * n : 256 * n + 256])
        for g in range(GROUPS):
            for h in range(2):
                qps[4 * g + 2 * n + h] = part[48 * g : 48 * g + 48, 128 * h : 128 * h + 128]

        def send_part(i, carry):
            g = lax.rem(gx + i // 2, GROUPS)
            head = 2 * n + lax.rem(i, 2)
            away = (g != gx) | (head != sa)

            @pl.when(away)
            def _():
                remote(
                    qps.at[4 * g + head], qpr.at[4 * gx + sa],
                    qp_s.at[4 * g + head], qp_r.at[4 * gx + sa], (g, gy, head),
                ).start()

            return carry

        lax.fori_loop(0, 8, send_part, 0)
    loads[1].wait()
    part = dot(xn[...], wkv[...])
    for g in range(GROUPS):
        kps[g] = part[48 * g : 48 * g + 48, :]
    for k in range(1, GROUPS):
        g = lax.rem(gx + k, GROUPS)
        remote(kps.at[g], kpr.at[gx], kp_s.at[g], kp_r.at[gx], (g, gy, sa)).start()
    qpr[4 * gx + sa] = qps[4 * gx + sa]
    kpr[gx] = kps[gx]

    def rotate(value, cos, sin):
        return value * cos + pltpu.roll(value, HEAD // 2, 1) * sin

    drain(ohr.at[pl.ds(0, PEERS - 1)], oh_r)

    def wait_part(i, carry):
        @pl.when(i != 4 * gx + sa)
        def _():
            drain(qpr.at[i], qp_r.at[i])

        return carry

    lax.fori_loop(0, 16, wait_part, 0)
    for t in range(STEPS):
        q = qpr[t] + qpr[4 + t] + qpr[8 + t] + qpr[12 + t]
        q = q.astype(bf16).astype(f32)
        at = slice(HEAD * t, HEAD * t + HEAD)
        qp[0:MEMBERS, at] = rotate(q, cos_ref[:, at], sin_ref[:, at]).astype(bf16)

    def send_query(k, carry):
        zd = lax.rem(z + z_offset(k), ZN)
        block = pl.ds(zd * 8, 8)
        pick = ohr[block].astype(f32).reshape(64, 128).astype(bf16)
        qsend[block] = dot(pick, qp[...]).reshape(8, SLOTS, 512).astype(bf16)

        def one(i, c):
            peer = zd * 8 + i

            @pl.when(peer != me)
            def _():
                remote(
                    qsend.at[peer], qrecv.at[me], q_s, q_r.at[z],
                    (gx, peer // 4, lax.rem(peer, 4)),
                ).start()

            return c

        return lax.fori_loop(0, 8, one, carry)

    lax.fori_loop(0, ZN, send_query, 0)
    qrecv[me] = qsend[me]

    def wait_kv(i, carry):
        @pl.when(i != gx)
        def _():
            drain(kpr.at[i], kp_r.at[i])

        return carry

    lax.fori_loop(0, GROUPS, wait_kv, 0)
    kv = (kpr[0] + kpr[1] + kpr[2] + kpr[3]).astype(bf16).astype(f32)
    turned = rotate(kv, cos_ref[:, lanes(sa)], sin_ref[:, lanes(sa)])
    kv = jnp.where(gy < KEY_VALUE_HEADS, turned, kv).astype(bf16)
    kvs[...] = kv
    appr[sa] = kv
    which = gy // 8
    target = lax.rem(gy, 8) * 2

    def send_new(i, carry):
        dgy = target + i // 4
        dsa = lax.rem(i, 4)
        away = (dgy != gy) | (dsa != sa)

        @pl.when(away)
        def _():
            remote(
                kvs, nkv.at[4 * which + sa], nk_s.at[i], nk_r.at[4 * which + sa],
                (gx, dgy, dsa),
            ).start()

        @pl.when(jnp.logical_not(away))
        def _():
            nkv[4 * which + sa] = kvs[...]

        return carry

    lax.fori_loop(0, 8, send_new, 0)
    for k in range(1, 4):
        remote(
            kvs, appr.at[sa], app_s.at[k - 1], app_r.at[sa], (gx, gy, lax.rem(sa + k, 4))
        ).start()

    loads[2].wait()
    loads[3].wait()
    scale = HEAD ** (-0.5)

    def attend(k, carry):
        j = lax.rem(z + ZN - z_offset(k), ZN)
        block = pl.ds(j * 8, 8)

        @pl.when(j == z)
        def _():
            drain(qrecv.at[pl.ds(0, 7)], q_r.at[j])

        @pl.when(j != z)
        def _():
            drain(qrecv.at[pl.ds(0, 8)], q_r.at[j])

        got = [
            qrecv[block, :, HEAD * t : HEAD * t + HEAD].astype(f32).reshape(64, HEAD)
            for t in range(STEPS)
        ]
        rows = dot(perm[...], jnp.concatenate(got, axis=0).astype(bf16)).astype(bf16)
        score = jnp.concatenate(
            [dot_nt(rows[32 * s : 32 * s + 32], kb[s, :, lanes(j)]) for s in range(SLOTS)], axis=0
        )
        mask = live[...]
        score = jnp.where(mask > 0.0, score * scale, neg_fill)
        top = jnp.max(score, axis=1, keepdims=True)
        weight = jnp.exp(score - top) * mask
        mass = jnp.sum(weight, axis=1, keepdims=True)
        weight = weight.astype(bf16)
        value = jnp.concatenate(
            [dot(weight[32 * s : 32 * s + 32], vb[s, :, lanes(j)]) for s in range(SLOTS)], axis=0
        )
        held = mass > 0.0
        mass = jnp.where(held, mass, 1.0)
        lse = jnp.where(held, top + jnp.log(mass), neg_fill)
        back = dot(permt[...], (value / mass).astype(bf16))
        for t in range(STEPS):
            osend[block, :, HEAD * t : HEAD * t + HEAD] = (
                back[64 * t : 64 * t + 64].reshape(8, SLOTS, HEAD).astype(bf16)
            )
        packed = jnp.zeros((8, 128), f32)
        for i in range(32):
            column = jnp.broadcast_to(lse[8 * i : 8 * i + 8], (8, 128))
            packed = jnp.where(lane8 == i, column, packed)
        for i in range(8):
            lsend[8 * j + i] = packed[i : i + 1]

        def one(i, c):
            peer = j * 8 + i

            @pl.when(peer != me)
            def _():
                dev = (gx, peer // 4, lax.rem(peer, 4))
                remote(osend.at[peer], orecv.at[me], o_s, o_r, dev).start()
                remote(lsend.at[peer], lrecv.at[me], l_s, l_r, dev).start()

            return c

        return lax.fori_loop(0, 8, one, carry)

    lax.fori_loop(0, ZN, attend, 0)
    orecv[me] = osend[me]
    lrecv[me] = lsend[me]

    def wait_new(i, carry):
        sgy = gy // 2 + 8 * (i // 4)

        @pl.when((sgy != gy) | (lax.rem(i, 4) != sa))
        def _():
            drain(nkv.at[i], nk_r.at[i])

        return carry

    lax.fori_loop(0, 8, wait_new, 0)
    fresh = {}
    for u in range(STEPS):
        q = qp[0:MEMBERS, HEAD * u : HEAD * u + HEAD].astype(f32)
        for v in range(u + 1):
            prod = q * nkv[v].astype(f32)
            fresh[u, v] = jnp.sum(prod, axis=1, keepdims=True) * scale
    for k in range(1, 4):
        src = lax.rem(sa + k, 4)
        drain(appr.at[src], app_r.at[src])
    for t in range(STEPS):
        app_ref[:, HEAD * t : HEAD * t + HEAD] = appr[t]

    held_by = dot_nt(
        (iota((MEMBERS, 128), 0) == iota((MEMBERS, 128), 1)).astype(f32).astype(bf16),
        ohr[...].astype(f32).reshape(512, 128).astype(bf16),
    )
    mine = held_by > 0.5

    drain(lrecv.at[pl.ds(0, PEERS - 1)], l_r)
    spread = jnp.broadcast_to(lrecv[...], (PEERS, SLOTS, 128)).reshape(512, 128)
    slot_of = iota((512, 128), 0) & 7
    lane512 = iota((512, 128), 1)
    table = jnp.zeros((512, 128), f32)
    for t in range(STEPS):
        column = jnp.sum(
            jnp.where(lane512 == slot_of * 4 + t, spread, 0.0), axis=1, keepdims=True
        )
        table = jnp.where(lane512 == t, column, table)
    table = jnp.transpose(table)
    drain(orecv.at[pl.ds(0, PEERS - 1)], o_r)
    for t in range(STEPS):
        lse = jnp.where(mine, table[t : t + 1, :], neg_fill)
        top = jnp.max(lse, axis=1, keepdims=True)
        for v in range(t + 1):
            top = jnp.maximum(top, fresh[t, v])
        weight = jnp.exp(lse - top)
        mass = jnp.sum(weight, axis=1, keepdims=True)
        high = weight.astype(bf16)
        low = (weight - high.astype(f32)).astype(bf16)
        pages = (
            orecv[:, :, HEAD * t : HEAD * t + HEAD].astype(f32).reshape(512, HEAD).astype(bf16)
        )
        value = dot(high, pages) + dot(low, pages)
        for v in range(t + 1):
            w = jnp.exp(fresh[t, v] - top)
            mass = mass + w
            value = value + w * nkv[4 + v].astype(f32)
        asend[t] = (value / mass).astype(bf16)

    def send_head(i, carry):
        g = lax.rem(gx + i // 4, GROUPS)
        t = lax.rem(sa + lax.rem(i, 4), 4)
        away = (g != gx) | (t != sa)

        @pl.when(away)
        def _():
            remote(
                asend.at[t], arecv.at[gx, :, lanes(sa)], a_s.at[4 * g + t],
                a_r.at[4 * gx + sa], (g, gy, t),
            ).start()

        @pl.when(jnp.logical_not(away))
        def _():
            arecv[gx, :, lanes(sa)] = asend[sa]

        return carry

    lax.fori_loop(0, 16, send_head, 0)
    loads[4].wait()

    def wait_head(i, carry):
        @pl.when(i != 4 * gx + sa)
        def _():
            drain(arecv.at[i // 4, :, lanes(lax.rem(i, 4))], a_r.at[i])

        return carry

    lax.fori_loop(0, 16, wait_head, 0)
    partner = (gx, gy + 1 - 2 * core, sa)
    first = core == 0

    def product(k, carry):
        zd = lax.rem(z + z_offset(ZN - 1 - k), ZN)
        part = dot(
            arecv[...].reshape(ROWS, 512), wo[:, pl.ds(pl.multiple_of(zd * 256, 256), 256)]
        )
        a, b = part[:, 0:128], part[:, 128:256]
        acc[zd] = jnp.where(first, a, b)
        psend[zd] = jnp.where(first, b, a)
        remote(psend.at[zd], precv.at[zd], p_s.at[zd], p_r.at[zd], partner).start()
        return carry

    lax.fori_loop(0, ZN, product, 0)

    def chip_sum(k, carry):
        zd = lax.rem(z + z_offset(ZN - 1 - k), ZN)
        drain(precv.at[zd], p_r.at[zd])
        both = acc[zd] + precv[zd]

        @pl.when(zd != z)
        def _():
            zsend[zd] = both.astype(bf16)
            remote(
                zsend.at[zd], zrecv.at[z], z_s.at[zd], z_r.at[z], (gx, 2 * zd + core, sa)
            ).start()

        @pl.when(zd == z)
        def _():
            acc[zd] = both

        return carry

    lax.fori_loop(0, ZN, chip_sum, 0)

    def gather_sum(k, carry):
        src = lax.rem(z + k, ZN)
        drain(zrecv.at[src], z_r.at[src])
        acc[z] += zrecv[src].astype(f32)
        return carry

    lax.fori_loop(1, ZN, gather_sum, 0)
    out_ref[sa] = acc[z]
    for k in range(1, 4):
        remote(
            out_ref.at[sa], out_ref.at[sa], x_s.at[k - 1], x_r.at[sa],
            (gx, gy, lax.rem(sa + k, 4)),
        ).start()
    for k in range(1, 4):
        src = lax.rem(sa + k, 4)
        drain(out_ref.at[src], x_r.at[src])

    for k in range(3):
        drain(sqs.at[gx], sq_s.at[k])
        drain(kvs, app_s.at[k])
        drain(out_ref.at[sa], x_s.at[k])
    drain(ohr.at[pl.ds(0, PEERS - 1)], oh_s)
    drain(qsend.at[pl.ds(0, PEERS - 1)], q_s)
    drain(osend.at[pl.ds(0, PEERS - 1)], o_s)
    drain(lsend.at[pl.ds(0, PEERS - 1)], l_s)

    def sent16(i, carry):
        @pl.when(i != 4 * gx + sa)
        def _():
            drain(qps.at[i], qp_s.at[i])
            drain(asend.at[0], a_s.at[i])

        return carry

    lax.fori_loop(0, 16, sent16, 0)

    def sent8(i, carry):
        drain(psend.at[i], p_s.at[i])

        @pl.when((target + i // 4 != gy) | (lax.rem(i, 4) != sa))
        def _():
            drain(kvs, nk_s.at[i])

        @pl.when(i != z)
        def _():
            drain(zsend.at[i], z_s.at[i])

        return carry

    lax.fori_loop(0, 8, sent8, 0)

    def sent4(i, carry):
        @pl.when(i != gx)
        def _():
            drain(kps.at[i], kp_s.at[i])

        return carry

    lax.fori_loop(0, GROUPS, sent4, 0)


def local(
    tokens, norm_gain, w_query, w_keyval, w_out,
    paged_key_cache, paged_value_cache, lengths, slot_owner, slot_page_number,
):
    gx = lax.axis_index("gx")
    sa = lax.axis_index("sa")
    x = lax.dynamic_index_in_dim(tokens, sa, 1, keepdims=False)
    group_lengths = lax.dynamic_slice_in_dim(lengths, gx * MEMBERS, MEMBERS)
    lane = jnp.arange(STEPS * HEAD, dtype=jnp.int32)
    exponent = (lane % (HEAD // 2)).astype(f32) * (-2.0 / HEAD)
    inverse_freq = jnp.power(f32(rope_base), exponent)
    angles = (group_lengths[:, None] + lane[None, :] // HEAD).astype(f32) * inverse_freq[None, :]
    cosine = jnp.cos(angles)
    sine = jnp.sin(angles)
    sine = jnp.where(lane[None, :] % HEAD < HEAD // 2, -sine, sine)

    vmem = pl.BlockSpec(memory_space=pltpu.VMEM)
    smem = pl.BlockSpec(memory_space=pltpu.SMEM)
    hbm = pl.BlockSpec(memory_space=pl.ANY)
    dma = pltpu.SemaphoreType.DMA
    V = pltpu.VMEM
    mixed, appended = pl.pallas_call(
        kernel,
        out_shape=(
            jax.ShapeDtypeStruct((STEPS, ROWS, HEAD), f32),
            jax.ShapeDtypeStruct((MEMBERS, STEPS * HEAD), bf16),
        ),
        in_specs=[vmem] * 4 + [smem] * 3 + [hbm] * 5,
        out_specs=(vmem, vmem),
        scratch_shapes=[
            V((2048, 512), bf16), V((2048, 128), bf16), V((512, 2048), bf16),
            V((SLOTS, PAGE, 1024), bf16), V((SLOTS, PAGE, 1024), bf16),
            V((ROWS, 2048), bf16), V((ROWS, 128), f32), V((GROUPS, 1, 256), f32),
            V((SLOTS, 128), bf16), V((PEERS, SLOTS, 128), bf16), V((256, 128), f32),
            V((256, 256), bf16), V((256, 256), bf16),
            V((16, MEMBERS, HEAD), f32), V((16, MEMBERS, HEAD), f32),
            V((GROUPS, MEMBERS, HEAD), f32), V((GROUPS, MEMBERS, HEAD), f32),
            V((128, 512), bf16),
            V((PEERS, SLOTS, 512), bf16), V((PEERS, SLOTS, 512), bf16),
            V((MEMBERS, HEAD), bf16), V((4, MEMBERS, HEAD), bf16), V((8, MEMBERS, HEAD), bf16),
            V((PEERS, SLOTS, 512), bf16), V((PEERS, SLOTS, 512), bf16),
            V((PEERS, 1, 128), f32), V((PEERS, 1, 128), f32),
            V((STEPS, MEMBERS, HEAD), bf16), V((GROUPS, MEMBERS, 512), bf16),
            V((ZN, ROWS, HEAD), f32), V((ZN, ROWS, HEAD), f32), V((ZN, ROWS, HEAD), f32),
            V((ZN, ROWS, HEAD), bf16), V((ZN, ROWS, HEAD), bf16),
            dma((5,)), dma((3,)), dma((4,)), dma, dma, dma((16,)), dma((16,)), dma((4,)),
            dma((4,)), dma, dma((8,)), dma((3,)), dma((4,)), dma((8,)), dma((8,)),
            dma, dma, dma, dma, dma((16,)), dma((16,)), dma((8,)), dma((8,)), dma((8,)),
            dma((8,)), dma((3,)), dma((4,)),
        ],
        compiler_params=pltpu.CompilerParams(
            collective_id=0, has_side_effects=True, vmem_limit_bytes=60 * 1024 * 1024
        ),
        name="paged_attention_layer",
    )(
        x, norm_gain.reshape(1, -1), cosine, sine, lengths, slot_owner, slot_page_number,
        w_query, w_keyval, w_out, paged_key_cache, paged_value_cache,
    )
    return (
        jnp.transpose(mixed, (1, 0, 2)),
        appended.reshape(MEMBERS, STEPS, HEAD),
    )


def solution(mesh):
    in_specs = (
        P(None, None, "gx"),
        P("gx"),
        P("gx", "gy"),
        P("gx", "gy"),
        P("gy", "gx"),
        P(("gx", "gy", "sa"), None, None),
        P(("gx", "gy", "sa"), None, None),
        P(),
        P(("gx", "gy", "sa")),
        P(("gx", "gy", "sa")),
    )
    out_specs = (P(None, None, ("gx", "gy")), P("gx", None, "gy"))
    return jax.shard_map(local, mesh=mesh, in_specs=in_specs, out_specs=out_specs, check_vma=False)
```

```python
import jax
import jax.numpy as jnp
from jax import lax
from jax.experimental import pallas as pl
from jax.experimental.pallas import tpu as pltpu
from jax.sharding import PartitionSpec as P

D = 8192
QUERY_HEADS = 64
KEY_VALUE_HEADS = 8
HEAD = 128
GROUPS = 4
MEMBERS = 48
STEPS = 4
SLOTS = 8
PAGE = 128
PEERS = 64
ZN = 8
ROWS = GROUPS * MEMBERS

rope_base = 500000.0
norm_eps = 1e-05
neg_fill = -1e30
MESH = pl.DeviceIdType.MESH
f32 = jnp.float32
bf16 = jnp.bfloat16


def dot(a, b):
    return jnp.dot(a, b, preferred_element_type=f32)


def dot_nt(a, b):
    return lax.dot_general(a, b, (((1,), (1,)), ((), ())), preferred_element_type=f32)


def iota(shape, axis):
    return lax.broadcasted_iota(jnp.int32, shape, axis)


def lanes(index):
    return pl.ds(pl.multiple_of(index * HEAD, HEAD), HEAD)


def z_offset(k):
    return jnp.where(lax.rem(k, 2) == 1, (k + 1) // 2, lax.rem(ZN - k // 2, ZN))


def drain(ref, sem):
    pltpu.make_async_copy(ref, ref, sem).wait()


def kernel(
    x_ref, gain_ref, cos_ref, sin_ref, len_ref, own_ref, page_ref,
    wq_hbm, wkv_hbm, wo_hbm, k_hbm, v_hbm,
    out_ref, app_ref, xrecv, gain_row,
    wq, wkv, wo, kb, vb, xn, sqcol, sqs, ohs, ohr, live, perm, permt,
    qps, qpr, kps, kpr, qp, qsend, qrecv, kvs, appr, nkv, osend, orecv,
    lsend, lrecv, asend, arecv, acc, psend, precv, zsend, zrecv,
    load_sem, sq_s, sq_r, oh_s, oh_r, qp_s, qp_r, kp_s, kp_r, q_s, q_r,
    app_s, app_r, nk_s, nk_r, o_s, o_r, l_s, l_r, a_s, a_r,
    p_s, p_r, z_s, z_r, x_s, x_r,
):
    gx = lax.axis_index("gx")
    gy = lax.axis_index("gy")
    sa = lax.axis_index("sa")
    z = gy // 2
    core = lax.rem(gy, 2)
    me = gy * 4 + sa

    def remote(src, dst, ss, rs, dev):
        return pltpu.make_async_remote_copy(
            src_ref=src, dst_ref=dst, send_sem=ss, recv_sem=rs,
            device_id=dev, device_id_type=MESH,
        )

    loads = [
        pltpu.make_async_copy(a, b, load_sem.at[i])
        for i, (a, b) in enumerate(
            [(wq_hbm, wq), (wkv_hbm, wkv), (k_hbm, kb), (v_hbm, vb), (wo_hbm, wo)]
        )
    ]
    for c in loads:
        c.start()

    barrier = pltpu.get_barrier_semaphore()

    def greet(k, carry):
        peer = lax.rem(me + k, PEERS)
        pl.semaphore_signal(
            barrier, inc=1, device_id=(gx, peer // 4, lax.rem(peer, 4)), device_id_type=MESH
        )
        return carry

    lax.fori_loop(1, PEERS, greet, 0)

    def greet_y(k, carry):
        pl.semaphore_signal(
            barrier, inc=1,
            device_id=(lax.rem(gx + 1 + k // 4, GROUPS), gy, lax.rem(k, 4)),
            device_id_type=MESH,
        )
        return carry

    lax.fori_loop(0, 12, greet_y, 0)

    gain = gain_ref[...].astype(f32)
    gain_row[...] = jnp.concatenate([gain[c : c + 1] for c in range(16)], axis=1)

    def square(i, carry):
        rows = pl.ds(pl.multiple_of(i * 16, 16), 16)
        xf = x_ref[rows, :].astype(f32)
        s = jnp.sum(xf * xf, axis=1, keepdims=True)
        sqcol[rows, :] = jnp.broadcast_to(s, (16, 128))
        return carry

    lax.fori_loop(0, ROWS // 16, square, 0)
    row128 = iota((128, 128), 0)
    lane128 = iota((128, 128), 1)
    eye = row128 == lane128
    r0 = jnp.sum(jnp.where(eye, sqcol[0:128, :], 0.0), axis=0, keepdims=True)
    r1 = jnp.sum(jnp.where(eye[0:64, :], sqcol[128:192, :], 0.0), axis=0, keepdims=True)
    sqs[gx, :, 0:128] = r0
    sqs[gx, :, 128:256] = r1

    row8 = iota((SLOTS, 128), 0)
    lane8 = iota((SLOTS, 128), 1)
    owner = jnp.zeros((SLOTS, 128), jnp.int32)
    for s in range(SLOTS):
        who = own_ref[s]
        page = page_ref[s]
        left = jnp.where(page >= 0, len_ref[who] - page * PAGE, 0)
        live[pl.ds(32 * s, 32), :] = (iota((32, 128), 1) < left).astype(f32)
        owner = jnp.where(row8 == s, who - gx * MEMBERS, owner)
    onehot = (lane8 == owner).astype(f32).astype(bf16)
    ohs[...] = onehot
    ohr[me] = onehot

    pl.semaphore_wait(barrier, PEERS - 1 + 12)

    for k in range(1, GROUPS):
        remote(
            sqs.at[gx], sqs.at[gx], sq_s.at[k - 1], sq_r.at[gx],
            (lax.rem(gx + k, GROUPS), gy, sa),
        ).start()

    def send_owner(k, carry):
        peer = lax.rem(me + k, PEERS)
        remote(ohs, ohr.at[me], oh_s, oh_r, (gx, peer // 4, lax.rem(peer, 4))).start()
        return carry

    lax.fori_loop(1, PEERS, send_owner, 0)

    pr = iota((256, 256), 0)
    pc = iota((256, 256), 1)
    want = ((pr >> 3) & 3) * 64 + (pr & 7) * 8 + (pr >> 5)
    perm[...] = (pc == want).astype(f32).astype(bf16)
    want = (pr & 7) * 32 + (pr >> 6) * 8 + ((pr >> 3) & 7)
    permt[...] = (pc == want).astype(f32).astype(bf16)
    qp[...] = jnp.zeros_like(qp)

    for k in range(1, GROUPS):
        src = lax.rem(gx + k, GROUPS)
        drain(sqs.at[src], sq_r.at[src])
    total = sqs[0] + sqs[1] + sqs[2] + sqs[3]
    t0 = jnp.broadcast_to(total[:, 0:128], (128, 128))
    t1 = jnp.broadcast_to(total[:, 128:256], (64, 128))
    c0 = jnp.sum(jnp.where(eye, t0, 0.0), axis=1, keepdims=True)
    c1 = jnp.sum(jnp.where(eye[0:64, :], t1, 0.0), axis=1, keepdims=True)
    sqcol[0:128, :] = jnp.broadcast_to(lax.rsqrt(c0 / D + norm_eps), (128, 128))
    sqcol[128:192, :] = jnp.broadcast_to(lax.rsqrt(c1 / D + norm_eps), (64, 128))

    def normalise(i, carry):
        rows = pl.ds(pl.multiple_of(i * 16, 16), 16)
        inv = sqcol[rows, 0:1]
        xf = x_ref[rows, :].astype(f32)
        xn[rows, :] = (xf * inv * gain_row[...]).astype(bf16)
        return carry

    lax.fori_loop(0, ROWS // 16, normalise, 0)

    loads[0].wait()
    for n in range(2):
        part = dot(xn[...], wq[:, 256 * n : 256 * n + 256])
        for g in range(GROUPS):
            for h in range(2):
                qps[4 * g + 2 * n + h] = part[48 * g : 48 * g + 48, 128 * h : 128 * h + 128]

        def send_part(i, carry):
            g = lax.rem(gx + i // 2, GROUPS)
            head = 2 * n + lax.rem(i, 2)
            away = (g != gx) | (head != sa)

            @pl.when(away)
            def _():
                remote(
                    qps.at[4 * g + head], qpr.at[4 * gx + sa],
                    qp_s.at[4 * g + head], qp_r.at[4 * gx + sa], (g, gy, head),
                ).start()

            return carry

        lax.fori_loop(0, 8, send_part, 0)
    loads[1].wait()
    part = dot(xn[...], wkv[...])
    for g in range(GROUPS):
        kps[g] = part[48 * g : 48 * g + 48, :]
    for k in range(1, GROUPS):
        g = lax.rem(gx + k, GROUPS)
        remote(kps.at[g], kpr.at[gx], kp_s.at[g], kp_r.at[gx], (g, gy, sa)).start()
    qpr[4 * gx + sa] = qps[4 * gx + sa]
    kpr[gx] = kps[gx]

    def rotate(value, cos, sin):
        return value * cos + pltpu.roll(value, HEAD // 2, 1) * sin

    drain(ohr.at[pl.ds(0, PEERS - 1)], oh_r)

    def wait_part(i, carry):
        @pl.when(i != 4 * gx + sa)
        def _():
            drain(qpr.at[i], qp_r.at[i])

        return carry

    lax.fori_loop(0, 16, wait_part, 0)
    for t in range(STEPS):
        q = qpr[t] + qpr[4 + t] + qpr[8 + t] + qpr[12 + t]
        q = q.astype(bf16).astype(f32)
        at = slice(HEAD * t, HEAD * t + HEAD)
        qp[0:MEMBERS, at] = rotate(q, cos_ref[:, at], sin_ref[:, at]).astype(bf16)

    def send_query(k, carry):
        zd = lax.rem(z + z_offset(k), ZN)
        block = pl.ds(zd * 8, 8)
        pick = ohr[block].astype(f32).reshape(64, 128).astype(bf16)
        qsend[block] = dot(pick, qp[...]).reshape(8, SLOTS, 512).astype(bf16)

        def one(i, c):
            peer = zd * 8 + i

            @pl.when(peer != me)
            def _():
                remote(
                    qsend.at[peer], qrecv.at[me], q_s, q_r.at[z],
                    (gx, peer // 4, lax.rem(peer, 4)),
                ).start()

            return c

        return lax.fori_loop(0, 8, one, carry)

    lax.fori_loop(0, ZN, send_query, 0)
    qrecv[me] = qsend[me]

    def wait_kv(i, carry):
        @pl.when(i != gx)
        def _():
            drain(kpr.at[i], kp_r.at[i])

        return carry

    lax.fori_loop(0, GROUPS, wait_kv, 0)
    kv = (kpr[0] + kpr[1] + kpr[2] + kpr[3]).astype(bf16).astype(f32)
    turned = rotate(kv, cos_ref[:, lanes(sa)], sin_ref[:, lanes(sa)])
    kv = jnp.where(gy < KEY_VALUE_HEADS, turned, kv).astype(bf16)
    kvs[...] = kv
    appr[sa] = kv
    which = gy // 8
    target = lax.rem(gy, 8) * 2

    def send_new(i, carry):
        dgy = target + i // 4
        dsa = lax.rem(i, 4)
        away = (dgy != gy) | (dsa != sa)

        @pl.when(away)
        def _():
            remote(
                kvs, nkv.at[4 * which + sa], nk_s.at[i], nk_r.at[4 * which + sa],
                (gx, dgy, dsa),
            ).start()

        @pl.when(jnp.logical_not(away))
        def _():
            nkv[4 * which + sa] = kvs[...]

        return carry

    lax.fori_loop(0, 8, send_new, 0)
    for k in range(1, 4):
        remote(
            kvs, appr.at[sa], app_s.at[k - 1], app_r.at[sa], (gx, gy, lax.rem(sa + k, 4))
        ).start()

    loads[2].wait()
    loads[3].wait()
    scale = HEAD ** (-0.5)

    def attend(k, carry):
        j = lax.rem(z + ZN - z_offset(k), ZN)
        block = pl.ds(j * 8, 8)

        @pl.when(j == z)
        def _():
            drain(qrecv.at[pl.ds(0, 7)], q_r.at[j])

        @pl.when(j != z)
        def _():
            drain(qrecv.at[pl.ds(0, 8)], q_r.at[j])

        got = [
            qrecv[block, :, HEAD * t : HEAD * t + HEAD].astype(f32).reshape(64, HEAD)
            for t in range(STEPS)
        ]
        rows = dot(perm[...], jnp.concatenate(got, axis=0).astype(bf16)).astype(bf16)
        score = jnp.concatenate(
            [dot_nt(rows[32 * s : 32 * s + 32], kb[s, :, lanes(j)]) for s in range(SLOTS)], axis=0
        )
        mask = live[...]
        score = jnp.where(mask > 0.0, score * scale, neg_fill)
        top = jnp.max(score, axis=1, keepdims=True)
        weight = jnp.exp(score - top) * mask
        mass = jnp.sum(weight, axis=1, keepdims=True)
        weight = weight.astype(bf16)
        value = jnp.concatenate(
            [dot(weight[32 * s : 32 * s + 32], vb[s, :, lanes(j)]) for s in range(SLOTS)], axis=0
        )
        held = mass > 0.0
        mass = jnp.where(held, mass, 1.0)
        lse = jnp.where(held, top + jnp.log(mass), neg_fill)
        back = dot(permt[...], (value / mass).astype(bf16))
        for t in range(STEPS):
            osend[block, :, HEAD * t : HEAD * t + HEAD] = (
                back[64 * t : 64 * t + 64].reshape(8, SLOTS, HEAD).astype(bf16)
            )
        packed = jnp.zeros((8, 128), f32)
        for i in range(32):
            column = jnp.broadcast_to(lse[8 * i : 8 * i + 8], (8, 128))
            packed = jnp.where(lane8 == i, column, packed)
        for i in range(8):
            lsend[8 * j + i] = packed[i : i + 1]

        def one(i, c):
            peer = j * 8 + i

            @pl.when(peer != me)
            def _():
                dev = (gx, peer // 4, lax.rem(peer, 4))
                remote(osend.at[peer], orecv.at[me], o_s, o_r, dev).start()
                remote(lsend.at[peer], lrecv.at[me], l_s, l_r, dev).start()

            return c

        return lax.fori_loop(0, 8, one, carry)

    lax.fori_loop(0, ZN, attend, 0)
    orecv[me] = osend[me]
    lrecv[me] = lsend[me]

    def wait_new(i, carry):
        sgy = gy // 2 + 8 * (i // 4)

        @pl.when((sgy != gy) | (lax.rem(i, 4) != sa))
        def _():
            drain(nkv.at[i], nk_r.at[i])

        return carry

    lax.fori_loop(0, 8, wait_new, 0)
    fresh = {}
    for u in range(STEPS):
        q = qp[0:MEMBERS, HEAD * u : HEAD * u + HEAD].astype(f32)
        for v in range(u + 1):
            prod = q * nkv[v].astype(f32)
            fresh[u, v] = jnp.sum(prod, axis=1, keepdims=True) * scale
    for k in range(1, 4):
        src = lax.rem(sa + k, 4)
        drain(appr.at[src], app_r.at[src])
    ar = iota((ROWS, ROWS), 0)
    weave = iota((ROWS, ROWS), 1) == (ar & 3) * MEMBERS + (ar >> 2)
    app_ref[...] = dot(
        weave.astype(f32).astype(bf16), appr[...].reshape(STEPS * MEMBERS, HEAD)
    ).astype(bf16)

    held_by = dot_nt(
        (iota((MEMBERS, 128), 0) == iota((MEMBERS, 128), 1)).astype(f32).astype(bf16),
        ohr[...].astype(f32).reshape(512, 128).astype(bf16),
    )
    mine = held_by > 0.5

    drain(lrecv.at[pl.ds(0, PEERS - 1)], l_r)
    spread = jnp.broadcast_to(lrecv[...], (PEERS, SLOTS, 128)).reshape(512, 128)
    slot_of = iota((512, 128), 0) & 7
    lane512 = iota((512, 128), 1)
    table = jnp.zeros((512, 128), f32)
    for t in range(STEPS):
        column = jnp.sum(
            jnp.where(lane512 == slot_of * 4 + t, spread, 0.0), axis=1, keepdims=True
        )
        table = jnp.where(lane512 == t, column, table)
    table = jnp.transpose(table)
    drain(orecv.at[pl.ds(0, PEERS - 1)], o_r)
    for t in range(STEPS):
        lse = jnp.where(mine, table[t : t + 1, :], neg_fill)
        top = jnp.max(lse, axis=1, keepdims=True)
        for v in range(t + 1):
            top = jnp.maximum(top, fresh[t, v])
        weight = jnp.exp(lse - top)
        mass = jnp.sum(weight, axis=1, keepdims=True)
        high = weight.astype(bf16)
        low = (weight - high.astype(f32)).astype(bf16)
        pages = (
            orecv[:, :, HEAD * t : HEAD * t + HEAD].astype(f32).reshape(512, HEAD).astype(bf16)
        )
        value = dot(high, pages) + dot(low, pages)
        for v in range(t + 1):
            w = jnp.exp(fresh[t, v] - top)
            mass = mass + w
            value = value + w * nkv[4 + v].astype(f32)
        asend[t] = (value / mass).astype(bf16)

    def send_head(i, carry):
        g = lax.rem(gx + i // 4, GROUPS)
        t = lax.rem(sa + lax.rem(i, 4), 4)
        away = (g != gx) | (t != sa)

        @pl.when(away)
        def _():
            remote(
                asend.at[t], arecv.at[gx, :, lanes(sa)], a_s.at[4 * g + t],
                a_r.at[4 * gx + sa], (g, gy, t),
            ).start()

        @pl.when(jnp.logical_not(away))
        def _():
            arecv[gx, :, lanes(sa)] = asend[sa]

        return carry

    lax.fori_loop(0, 16, send_head, 0)
    loads[4].wait()

    def wait_head(i, carry):
        @pl.when(i != 4 * gx + sa)
        def _():
            drain(arecv.at[i // 4, :, lanes(lax.rem(i, 4))], a_r.at[i])

        return carry

    lax.fori_loop(0, 16, wait_head, 0)
    partner = (gx, gy + 1 - 2 * core, sa)
    first = core == 0

    def product(k, carry):
        zd = lax.rem(z + z_offset(ZN - 1 - k), ZN)
        part = dot(
            arecv[...].reshape(ROWS, 512), wo[:, pl.ds(pl.multiple_of(zd * 256, 256), 256)]
        )
        a, b = part[:, 0:128], part[:, 128:256]
        acc[zd] = jnp.where(first, a, b)
        psend[zd] = jnp.where(first, b, a)
        remote(psend.at[zd], precv.at[zd], p_s.at[zd], p_r.at[zd], partner).start()

        @pl.when(k >= 2)
        def _():
            chip_sum(k - 2, 0)

        return carry

    def chip_sum(k, carry):
        zd = lax.rem(z + z_offset(ZN - 1 - k), ZN)
        drain(precv.at[zd], p_r.at[zd])
        both = acc[zd] + precv[zd]

        @pl.when(zd != z)
        def _():
            zsend[zd] = both.astype(bf16)
            remote(
                zsend.at[zd], zrecv.at[z], z_s.at[zd], z_r.at[z], (gx, 2 * zd + core, sa)
            ).start()

        @pl.when(zd == z)
        def _():
            acc[zd] = both

        return carry

    lax.fori_loop(0, ZN, product, 0)
    lax.fori_loop(ZN - 2, ZN, chip_sum, 0)

    def gather_sum(k, carry):
        src = lax.rem(z + k, ZN)
        drain(zrecv.at[src], z_r.at[src])
        acc[z] += zrecv[src].astype(f32)
        return carry

    lax.fori_loop(1, ZN, gather_sum, 0)
    xrecv[sa] = acc[z].astype(bf16)
    for k in range(1, 4):
        remote(
            xrecv.at[sa], xrecv.at[sa], x_s.at[k - 1], x_r.at[sa],
            (gx, gy, lax.rem(sa + k, 4)),
        ).start()
    for k in range(1, 4):
        src = lax.rem(sa + k, 4)
        drain(xrecv.at[src], x_r.at[src])
    for t in range(STEPS):
        out_ref[pl.ds(t, ROWS, stride=STEPS), :] = xrecv[t].astype(f32)

    for k in range(3):
        drain(sqs.at[gx], sq_s.at[k])
        drain(kvs, app_s.at[k])
        drain(xrecv.at[sa], x_s.at[k])
    drain(ohr.at[pl.ds(0, PEERS - 1)], oh_s)
    drain(qsend.at[pl.ds(0, PEERS - 1)], q_s)
    drain(osend.at[pl.ds(0, PEERS - 1)], o_s)
    drain(lsend.at[pl.ds(0, PEERS - 1)], l_s)

    def sent16(i, carry):
        @pl.when(i != 4 * gx + sa)
        def _():
            drain(qps.at[i], qp_s.at[i])
            drain(asend.at[0], a_s.at[i])

        return carry

    lax.fori_loop(0, 16, sent16, 0)

    def sent8(i, carry):
        drain(psend.at[i], p_s.at[i])

        @pl.when((target + i // 4 != gy) | (lax.rem(i, 4) != sa))
        def _():
            drain(kvs, nk_s.at[i])

        @pl.when(i != z)
        def _():
            drain(zsend.at[i], z_s.at[i])

        return carry

    lax.fori_loop(0, 8, sent8, 0)

    def sent4(i, carry):
        @pl.when(i != gx)
        def _():
            drain(kps.at[i], kp_s.at[i])

        return carry

    lax.fori_loop(0, GROUPS, sent4, 0)


def local(
    tokens, norm_gain, w_query, w_keyval, w_out,
    paged_key_cache, paged_value_cache, lengths, slot_owner, slot_page_number,
):
    gx = lax.axis_index("gx")
    sa = lax.axis_index("sa")
    x = lax.dynamic_index_in_dim(tokens, sa, 1, keepdims=False)
    group_lengths = lax.dynamic_slice_in_dim(lengths, gx * MEMBERS, MEMBERS)
    lane = jnp.arange(STEPS * HEAD, dtype=jnp.int32)
    exponent = (lane % (HEAD // 2)).astype(f32) * (-2.0 / HEAD)
    inverse_freq = jnp.power(f32(rope_base), exponent)
    angles = (group_lengths[:, None] + lane[None, :] // HEAD).astype(f32) * inverse_freq[None, :]
    cosine = jnp.cos(angles)
    sine = jnp.sin(angles)
    sine = jnp.where(lane[None, :] % HEAD < HEAD // 2, -sine, sine)

    vmem = pl.BlockSpec(memory_space=pltpu.VMEM)
    smem = pl.BlockSpec(memory_space=pltpu.SMEM)
    hbm = pl.BlockSpec(memory_space=pl.ANY)
    dma = pltpu.SemaphoreType.DMA
    V = pltpu.VMEM
    mixed, appended = pl.pallas_call(
        kernel,
        out_shape=(
            jax.ShapeDtypeStruct((STEPS * ROWS, HEAD), f32),
            jax.ShapeDtypeStruct((MEMBERS * STEPS, HEAD), bf16),
        ),
        in_specs=[vmem] * 4 + [smem] * 3 + [hbm] * 5,
        out_specs=(vmem, vmem),
        scratch_shapes=[
            V((STEPS, ROWS, HEAD), bf16), V((1, 2048), f32),
            V((2048, 512), bf16), V((2048, 128), bf16), V((512, 2048), bf16),
            V((SLOTS, PAGE, 1024), bf16), V((SLOTS, PAGE, 1024), bf16),
            V((ROWS, 2048), bf16), V((ROWS, 128), f32), V((GROUPS, 1, 256), f32),
            V((SLOTS, 128), bf16), V((PEERS, SLOTS, 128), bf16), V((256, 128), f32),
            V((256, 256), bf16), V((256, 256), bf16),
            V((16, MEMBERS, HEAD), f32), V((16, MEMBERS, HEAD), f32),
            V((GROUPS, MEMBERS, HEAD), f32), V((GROUPS, MEMBERS, HEAD), f32),
            V((128, 512), bf16),
            V((PEERS, SLOTS, 512), bf16), V((PEERS, SLOTS, 512), bf16),
            V((MEMBERS, HEAD), bf16), V((4, MEMBERS, HEAD), bf16), V((8, MEMBERS, HEAD), bf16),
            V((PEERS, SLOTS, 512), bf16), V((PEERS, SLOTS, 512), bf16),
            V((PEERS, 1, 128), f32), V((PEERS, 1, 128), f32),
            V((STEPS, MEMBERS, HEAD), bf16), V((GROUPS, MEMBERS, 512), bf16),
            V((ZN, ROWS, HEAD), f32), V((ZN, ROWS, HEAD), f32), V((ZN, ROWS, HEAD), f32),
            V((ZN, ROWS, HEAD), bf16), V((ZN, ROWS, HEAD), bf16),
            dma((5,)), dma((3,)), dma((4,)), dma, dma, dma((16,)), dma((16,)), dma((4,)),
            dma((4,)), dma, dma((8,)), dma((3,)), dma((4,)), dma((8,)), dma((8,)),
            dma, dma, dma, dma, dma((16,)), dma((16,)), dma((8,)), dma((8,)), dma((8,)),
            dma((8,)), dma((3,)), dma((4,)),
        ],
        compiler_params=pltpu.CompilerParams(
            collective_id=0, has_side_effects=True, vmem_limit_bytes=60 * 1024 * 1024
        ),
        name="paged_attention_layer",
    )(
        x, norm_gain.reshape(16, 128), cosine, sine, lengths, slot_owner, slot_page_number,
        w_query, w_keyval, w_out, paged_key_cache, paged_value_cache,
    )
    return (
        mixed.reshape(ROWS, STEPS, HEAD),
        appended.reshape(MEMBERS, STEPS, HEAD),
    )


def solution(mesh):
    in_specs = (
        P(None, None, "gx"),
        P("gx"),
        P("gx", "gy"),
        P("gx", "gy"),
        P("gy", "gx"),
        P(("gx", "gy", "sa"), None, None),
        P(("gx", "gy", "sa"), None, None),
        P(),
        P(("gx", "gy", "sa")),
        P(("gx", "gy", "sa")),
    )
    out_specs = (P(None, None, ("gx", "gy")), P("gx", None, "gy"))
    return jax.shard_map(local, mesh=mesh, in_specs=in_specs, out_specs=out_specs, check_vma=False)
```

```python
import jax
import jax.numpy as jnp
from jax import lax
from jax.experimental import pallas as pl
from jax.experimental.pallas import tpu as pltpu
from jax.sharding import PartitionSpec as P

D = 8192
QUERY_HEADS = 64
KEY_VALUE_HEADS = 8
HEAD = 128
GROUPS = 4
MEMBERS = 48
STEPS = 4
SLOTS = 8
PAGE = 128
PEERS = 64
ZN = 8
ROWS = GROUPS * MEMBERS

rope_base = 500000.0
norm_eps = 1e-05
neg_fill = -1e30
MESH = pl.DeviceIdType.MESH
f32 = jnp.float32
bf16 = jnp.bfloat16


def dot(a, b):
    return jnp.dot(a, b, preferred_element_type=f32)


def dot_nt(a, b):
    return lax.dot_general(a, b, (((1,), (1,)), ((), ())), preferred_element_type=f32)


def iota(shape, axis):
    return lax.broadcasted_iota(jnp.int32, shape, axis)


def lanes(index):
    return pl.ds(pl.multiple_of(index * HEAD, HEAD), HEAD)


def z_offset(k):
    return jnp.where(lax.rem(k, 2) == 1, (k + 1) // 2, lax.rem(ZN - k // 2, ZN))


def drain(ref, sem):
    pltpu.make_async_copy(ref, ref, sem).wait()


def kernel(
    x_ref, gain_ref, cos_ref, sin_ref, len_ref, own_ref, page_ref,
    wq_hbm, wkv_hbm, wo_hbm, k_hbm, v_hbm,
    out_ref, app_ref, xrecv, gain_row,
    wq, wkv, wo, kb, vb, xn, sqcol, sqs, ohs, ohr, live, perm, permt,
    qps, qpr, kps, kpr, qp, qsend, qrecv, kvs, appr, nkv, osend, orecv,
    asend, arecv, acc, psend, precv, zsend, zrecv,
    load_sem, sq_s, sq_r, oh_s, oh_r, qp_s, qp_r, kp_s, kp_r, q_s, q_r,
    app_s, app_r, nk_s, nk_r, o_s, o_r, a_s, a_r,
    p_s, p_r, z_s, z_r, x_s, x_r,
):
    gx = lax.axis_index("gx")
    gy = lax.axis_index("gy")
    sa = lax.axis_index("sa")
    z = gy // 2
    core = lax.rem(gy, 2)
    me = gy * 4 + sa

    def remote(src, dst, ss, rs, dev):
        return pltpu.make_async_remote_copy(
            src_ref=src, dst_ref=dst, send_sem=ss, recv_sem=rs,
            device_id=dev, device_id_type=MESH,
        )

    loads = [
        pltpu.make_async_copy(a, b, load_sem.at[i])
        for i, (a, b) in enumerate(
            [(wq_hbm, wq), (wkv_hbm, wkv), (k_hbm, kb), (v_hbm, vb), (wo_hbm, wo)]
        )
    ]
    for c in loads:
        c.start()

    barrier = pltpu.get_barrier_semaphore()

    def greet(k, carry):
        peer = lax.rem(me + k, PEERS)
        pl.semaphore_signal(
            barrier, inc=1, device_id=(gx, peer // 4, lax.rem(peer, 4)), device_id_type=MESH
        )
        return carry

    lax.fori_loop(1, PEERS, greet, 0)

    def greet_y(k, carry):
        pl.semaphore_signal(
            barrier, inc=1,
            device_id=(lax.rem(gx + 1 + k // 4, GROUPS), gy, lax.rem(k, 4)),
            device_id_type=MESH,
        )
        return carry

    lax.fori_loop(0, 12, greet_y, 0)

    gain = gain_ref[...].astype(f32)
    gain_row[...] = jnp.concatenate([gain[c : c + 1] for c in range(16)], axis=1)

    def square(i, carry):
        rows = pl.ds(pl.multiple_of(i * 16, 16), 16)
        xf = x_ref[rows, :].astype(f32)
        s = jnp.sum(xf * xf, axis=1, keepdims=True)
        sqcol[rows, :] = jnp.broadcast_to(s, (16, 128))
        return carry

    lax.fori_loop(0, ROWS // 16, square, 0)
    row128 = iota((128, 128), 0)
    lane128 = iota((128, 128), 1)
    eye = row128 == lane128
    r0 = jnp.sum(jnp.where(eye, sqcol[0:128, :], 0.0), axis=0, keepdims=True)
    r1 = jnp.sum(jnp.where(eye[0:64, :], sqcol[128:192, :], 0.0), axis=0, keepdims=True)
    sqs[gx, :, 0:128] = r0
    sqs[gx, :, 128:256] = r1

    row8 = iota((SLOTS, 128), 0)
    lane8 = iota((SLOTS, 128), 1)
    owner = jnp.zeros((SLOTS, 128), jnp.int32)
    for s in range(SLOTS):
        who = own_ref[s]
        page = page_ref[s]
        left = jnp.where(page >= 0, len_ref[who] - page * PAGE, 0)
        live[pl.ds(32 * s, 32), :] = (iota((32, 128), 1) < left).astype(f32)
        owner = jnp.where(row8 == s, who - gx * MEMBERS, owner)
    onehot = (lane8 == owner).astype(f32).astype(bf16)
    ohs[...] = onehot
    ohr[me] = onehot

    pl.semaphore_wait(barrier, PEERS - 1 + 12)

    for k in range(1, GROUPS):
        remote(
            sqs.at[gx], sqs.at[gx], sq_s.at[k - 1], sq_r.at[gx],
            (lax.rem(gx + k, GROUPS), gy, sa),
        ).start()

    def send_owner(k, carry):
        peer = lax.rem(me + k, PEERS)
        remote(ohs, ohr.at[me], oh_s, oh_r, (gx, peer // 4, lax.rem(peer, 4))).start()
        return carry

    lax.fori_loop(1, PEERS, send_owner, 0)

    pr = iota((256, 256), 0)
    pc = iota((256, 256), 1)
    want = ((pr >> 3) & 3) * 64 + (pr & 7) * 8 + (pr >> 5)
    perm[...] = (pc == want).astype(f32).astype(bf16)
    want = (pr & 7) * 32 + (pr >> 6) * 8 + ((pr >> 3) & 7)
    permt[...] = (pc == want).astype(f32).astype(bf16)
    qp[...] = jnp.zeros_like(qp)

    for k in range(1, GROUPS):
        src = lax.rem(gx + k, GROUPS)
        drain(sqs.at[src], sq_r.at[src])
    total = sqs[0] + sqs[1] + sqs[2] + sqs[3]
    t0 = jnp.broadcast_to(total[:, 0:128], (128, 128))
    t1 = jnp.broadcast_to(total[:, 128:256], (64, 128))
    c0 = jnp.sum(jnp.where(eye, t0, 0.0), axis=1, keepdims=True)
    c1 = jnp.sum(jnp.where(eye[0:64, :], t1, 0.0), axis=1, keepdims=True)
    sqcol[0:128, :] = jnp.broadcast_to(lax.rsqrt(c0 / D + norm_eps), (128, 128))
    sqcol[128:192, :] = jnp.broadcast_to(lax.rsqrt(c1 / D + norm_eps), (64, 128))

    def normalise(i, carry):
        rows = pl.ds(pl.multiple_of(i * 16, 16), 16)
        inv = sqcol[rows, 0:1]
        xf = x_ref[rows, :].astype(f32)
        xn[rows, :] = (xf * inv * gain_row[...]).astype(bf16)
        return carry

    lax.fori_loop(0, ROWS // 16, normalise, 0)

    loads[0].wait()
    for n in range(2):
        part = dot(xn[...], wq[:, 256 * n : 256 * n + 256])
        for g in range(GROUPS):
            for h in range(2):
                qps[4 * g + 2 * n + h] = part[48 * g : 48 * g + 48, 128 * h : 128 * h + 128]

        def send_part(i, carry):
            g = lax.rem(gx + i // 2, GROUPS)
            head = 2 * n + lax.rem(i, 2)
            away = (g != gx) | (head != sa)

            @pl.when(away)
            def _():
                remote(
                    qps.at[4 * g + head], qpr.at[4 * gx + sa],
                    qp_s.at[4 * g + head], qp_r.at[4 * gx + sa], (g, gy, head),
                ).start()

            return carry

        lax.fori_loop(0, 8, send_part, 0)
    loads[1].wait()
    part = dot(xn[...], wkv[...])
    for g in range(GROUPS):
        kps[g] = part[48 * g : 48 * g + 48, :]
    for k in range(1, GROUPS):
        g = lax.rem(gx + k, GROUPS)
        remote(kps.at[g], kpr.at[gx], kp_s.at[g], kp_r.at[gx], (g, gy, sa)).start()
    qpr[4 * gx + sa] = qps[4 * gx + sa]
    kpr[gx] = kps[gx]

    def rotate(value, cos, sin):
        return value * cos + pltpu.roll(value, HEAD // 2, 1) * sin

    drain(ohr.at[pl.ds(0, PEERS - 1)], oh_r)

    def wait_part(i, carry):
        @pl.when(i != 4 * gx + sa)
        def _():
            drain(qpr.at[i], qp_r.at[i])

        return carry

    lax.fori_loop(0, 16, wait_part, 0)
    for t in range(STEPS):
        q = qpr[t] + qpr[4 + t] + qpr[8 + t] + qpr[12 + t]
        q = q.astype(bf16).astype(f32)
        at = slice(HEAD * t, HEAD * t + HEAD)
        qp[0:MEMBERS, at] = rotate(q, cos_ref[:, at], sin_ref[:, at]).astype(bf16)

    def send_query(k, carry):
        zd = lax.rem(z + z_offset(k), ZN)
        block = pl.ds(zd * 8, 8)
        pick = ohr[block].astype(f32).reshape(64, 128).astype(bf16)
        qsend[block] = dot(pick, qp[...]).reshape(8, SLOTS, 512).astype(bf16)

        def one(i, c):
            peer = zd * 8 + i

            @pl.when(peer != me)
            def _():
                remote(
                    qsend.at[peer], qrecv.at[me], q_s, q_r.at[z],
                    (gx, peer // 4, lax.rem(peer, 4)),
                ).start()

            return c

        return lax.fori_loop(0, 8, one, carry)

    lax.fori_loop(0, ZN, send_query, 0)
    qrecv[me] = qsend[me]

    def wait_kv(i, carry):
        @pl.when(i != gx)
        def _():
            drain(kpr.at[i], kp_r.at[i])

        return carry

    lax.fori_loop(0, GROUPS, wait_kv, 0)
    kv = (kpr[0] + kpr[1] + kpr[2] + kpr[3]).astype(bf16).astype(f32)
    turned = rotate(kv, cos_ref[:, lanes(sa)], sin_ref[:, lanes(sa)])
    kv = jnp.where(gy < KEY_VALUE_HEADS, turned, kv).astype(bf16)
    kvs[...] = kv
    appr[sa] = kv
    which = gy // 8
    target = lax.rem(gy, 8) * 2

    def send_new(i, carry):
        dgy = target + i // 4
        dsa = lax.rem(i, 4)
        away = (dgy != gy) | (dsa != sa)

        @pl.when(away)
        def _():
            remote(
                kvs, nkv.at[4 * which + sa], nk_s.at[i], nk_r.at[4 * which + sa],
                (gx, dgy, dsa),
            ).start()

        @pl.when(jnp.logical_not(away))
        def _():
            nkv[4 * which + sa] = kvs[...]

        return carry

    lax.fori_loop(0, 8, send_new, 0)
    for k in range(1, 4):
        remote(
            kvs, appr.at[sa], app_s.at[k - 1], app_r.at[sa], (gx, gy, lax.rem(sa + k, 4))
        ).start()

    loads[2].wait()
    loads[3].wait()
    scale = HEAD ** (-0.5)

    def attend(k, carry):
        j = lax.rem(z + ZN - z_offset(k), ZN)
        block = pl.ds(j * 8, 8)

        @pl.when(j == z)
        def _():
            drain(qrecv.at[pl.ds(0, 7)], q_r.at[j])

        @pl.when(j != z)
        def _():
            drain(qrecv.at[pl.ds(0, 8)], q_r.at[j])

        got = [
            qrecv[block, :, HEAD * t : HEAD * t + HEAD].astype(f32).reshape(64, HEAD)
            for t in range(STEPS)
        ]
        rows = dot(perm[...], jnp.concatenate(got, axis=0).astype(bf16)).astype(bf16)
        score = jnp.concatenate(
            [dot_nt(rows[32 * s : 32 * s + 32], kb[s, :, lanes(j)]) for s in range(SLOTS)], axis=0
        )
        mask = live[...]
        score = jnp.where(mask > 0.0, score * scale, neg_fill)
        top = jnp.max(score, axis=1, keepdims=True)
        weight = jnp.exp(score - top) * mask
        mass = jnp.sum(weight, axis=1, keepdims=True)
        weight = weight.astype(bf16)
        value = jnp.concatenate(
            [dot(weight[32 * s : 32 * s + 32], vb[s, :, lanes(j)]) for s in range(SLOTS)], axis=0
        )
        held = mass > 0.0
        mass = jnp.where(held, mass, 1.0)
        lse = jnp.where(held, top + jnp.log(mass), neg_fill)
        high = lse.astype(bf16).astype(f32)
        middle = (lse - high).astype(bf16).astype(f32)
        low = lse - high - middle
        place = iota((256, 128), 1) - 3 * ((iota((256, 128), 0) >> 3) & 3)
        parts = jnp.where(
            place == 0, high, jnp.where(place == 1, middle, jnp.where(place == 2, low, 0.0))
        )
        sent = jnp.concatenate([(value / mass).astype(bf16), parts.astype(bf16)], axis=1)
        back = dot(permt[...], sent)
        extra = back[0:64, 128:] + back[64:128, 128:] + back[128:192, 128:] + back[192:, 128:]
        osend[block, :, STEPS * HEAD :] = extra.reshape(8, SLOTS, HEAD).astype(bf16)
        for t in range(STEPS):
            osend[block, :, HEAD * t : HEAD * t + HEAD] = (
                back[64 * t : 64 * t + 64, 0:128].reshape(8, SLOTS, HEAD).astype(bf16)
            )
        def one(i, c):
            peer = j * 8 + i

            @pl.when(peer != me)
            def _():
                dev = (gx, peer // 4, lax.rem(peer, 4))
                remote(osend.at[peer], orecv.at[me], o_s, o_r, dev).start()

            return c

        return lax.fori_loop(0, 8, one, carry)

    lax.fori_loop(0, ZN, attend, 0)
    orecv[me] = osend[me]

    def wait_new(i, carry):
        sgy = gy // 2 + 8 * (i // 4)

        @pl.when((sgy != gy) | (lax.rem(i, 4) != sa))
        def _():
            drain(nkv.at[i], nk_r.at[i])

        return carry

    lax.fori_loop(0, 8, wait_new, 0)
    fresh = {}
    for u in range(STEPS):
        q = qp[0:MEMBERS, HEAD * u : HEAD * u + HEAD].astype(f32)
        for v in range(u + 1):
            prod = q * nkv[v].astype(f32)
            fresh[u, v] = jnp.sum(prod, axis=1, keepdims=True) * scale
    for k in range(1, 4):
        src = lax.rem(sa + k, 4)
        drain(appr.at[src], app_r.at[src])
    ar = iota((ROWS, ROWS), 0)
    weave = iota((ROWS, ROWS), 1) == (ar & 3) * MEMBERS + (ar >> 2)
    app_ref[...] = dot(
        weave.astype(f32).astype(bf16), appr[...].reshape(STEPS * MEMBERS, HEAD)
    ).astype(bf16)

    held_by = dot_nt(
        (iota((MEMBERS, 128), 0) == iota((MEMBERS, 128), 1)).astype(f32).astype(bf16),
        ohr[...].astype(f32).reshape(512, 128).astype(bf16),
    )
    mine = held_by > 0.5

    drain(orecv.at[pl.ds(0, PEERS - 1)], o_r)
    table = jnp.transpose(orecv[:, :, STEPS * HEAD :].astype(f32).reshape(512, 128))
    for t in range(STEPS):
        lse = table[3 * t : 3 * t + 1] + table[3 * t + 1 : 3 * t + 2] + table[3 * t + 2 : 3 * t + 3]
        lse = jnp.where(mine, lse, neg_fill)
        top = jnp.max(lse, axis=1, keepdims=True)
        for v in range(t + 1):
            top = jnp.maximum(top, fresh[t, v])
        weight = jnp.exp(lse - top)
        mass = jnp.sum(weight, axis=1, keepdims=True)
        high = weight.astype(bf16)
        low = (weight - high.astype(f32)).astype(bf16)
        pages = (
            orecv[:, :, HEAD * t : HEAD * t + HEAD].astype(f32).reshape(512, HEAD).astype(bf16)
        )
        value = dot(high, pages) + dot(low, pages)
        for v in range(t + 1):
            w = jnp.exp(fresh[t, v] - top)
            mass = mass + w
            value = value + w * nkv[4 + v].astype(f32)
        asend[t] = (value / mass).astype(bf16)

    def send_head(i, carry):
        g = lax.rem(gx + i // 4, GROUPS)
        t = lax.rem(sa + lax.rem(i, 4), 4)
        away = (g != gx) | (t != sa)

        @pl.when(away)
        def _():
            remote(
                asend.at[t], arecv.at[gx, :, lanes(sa)], a_s.at[4 * g + t],
                a_r.at[4 * gx + sa], (g, gy, t),
            ).start()

        @pl.when(jnp.logical_not(away))
        def _():
            arecv[gx, :, lanes(sa)] = asend[sa]

        return carry

    lax.fori_loop(0, 16, send_head, 0)
    loads[4].wait()

    def wait_head(i, carry):
        @pl.when(i != 4 * gx + sa)
        def _():
            drain(arecv.at[i // 4, :, lanes(lax.rem(i, 4))], a_r.at[i])

        return carry

    lax.fori_loop(0, 16, wait_head, 0)
    partner = (gx, gy + 1 - 2 * core, sa)
    first = core == 0

    def product(k, carry):
        zd = lax.rem(z + z_offset(ZN - 1 - k), ZN)
        part = dot(
            arecv[...].reshape(ROWS, 512), wo[:, pl.ds(pl.multiple_of(zd * 256, 256), 256)]
        )
        a, b = part[:, 0:128], part[:, 128:256]
        acc[zd] = jnp.where(first, a, b)
        psend[zd] = jnp.where(first, b, a)
        remote(psend.at[zd], precv.at[zd], p_s.at[zd], p_r.at[zd], partner).start()

        @pl.when(k >= 2)
        def _():
            chip_sum(k - 2, 0)

        return carry

    def chip_sum(k, carry):
        zd = lax.rem(z + z_offset(ZN - 1 - k), ZN)
        drain(precv.at[zd], p_r.at[zd])
        both = acc[zd] + precv[zd]

        @pl.when(zd != z)
        def _():
            zsend[zd] = both.astype(bf16)
            remote(
                zsend.at[zd], zrecv.at[z], z_s.at[zd], z_r.at[z], (gx, 2 * zd + core, sa)
            ).start()

        @pl.when(zd == z)
        def _():
            acc[zd] = both

        return carry

    lax.fori_loop(0, ZN, product, 0)
    lax.fori_loop(ZN - 2, ZN, chip_sum, 0)

    def gather_sum(k, carry):
        src = lax.rem(z + k, ZN)
        drain(zrecv.at[src], z_r.at[src])
        acc[z] += zrecv[src].astype(f32)
        return carry

    lax.fori_loop(1, ZN, gather_sum, 0)
    xrecv[sa] = acc[z].astype(bf16)
    for k in range(1, 4):
        remote(
            xrecv.at[sa], xrecv.at[sa], x_s.at[k - 1], x_r.at[sa],
            (gx, gy, lax.rem(sa + k, 4)),
        ).start()
    for k in range(1, 4):
        src = lax.rem(sa + k, 4)
        drain(xrecv.at[src], x_r.at[src])
    for t in range(STEPS):
        out_ref[pl.ds(t, ROWS, stride=STEPS), :] = xrecv[t].astype(f32)

    for k in range(3):
        drain(sqs.at[gx], sq_s.at[k])
        drain(kvs, app_s.at[k])
        drain(xrecv.at[sa], x_s.at[k])
    drain(ohr.at[pl.ds(0, PEERS - 1)], oh_s)
    drain(qsend.at[pl.ds(0, PEERS - 1)], q_s)
    drain(osend.at[pl.ds(0, PEERS - 1)], o_s)

    def sent16(i, carry):
        @pl.when(i != 4 * gx + sa)
        def _():
            drain(qps.at[i], qp_s.at[i])
            drain(asend.at[0], a_s.at[i])

        return carry

    lax.fori_loop(0, 16, sent16, 0)

    def sent8(i, carry):
        drain(psend.at[i], p_s.at[i])

        @pl.when((target + i // 4 != gy) | (lax.rem(i, 4) != sa))
        def _():
            drain(kvs, nk_s.at[i])

        @pl.when(i != z)
        def _():
            drain(zsend.at[i], z_s.at[i])

        return carry

    lax.fori_loop(0, 8, sent8, 0)

    def sent4(i, carry):
        @pl.when(i != gx)
        def _():
            drain(kps.at[i], kp_s.at[i])

        return carry

    lax.fori_loop(0, GROUPS, sent4, 0)


def local(
    tokens, norm_gain, w_query, w_keyval, w_out,
    paged_key_cache, paged_value_cache, lengths, slot_owner, slot_page_number,
):
    gx = lax.axis_index("gx")
    sa = lax.axis_index("sa")
    x = lax.dynamic_index_in_dim(tokens, sa, 1, keepdims=False)
    group_lengths = lax.dynamic_slice_in_dim(lengths, gx * MEMBERS, MEMBERS)
    lane = jnp.arange(STEPS * HEAD, dtype=jnp.int32)
    exponent = (lane % (HEAD // 2)).astype(f32) * (-2.0 / HEAD)
    inverse_freq = jnp.power(f32(rope_base), exponent)
    angles = (group_lengths[:, None] + lane[None, :] // HEAD).astype(f32) * inverse_freq[None, :]
    cosine = jnp.cos(angles)
    sine = jnp.sin(angles)
    sine = jnp.where(lane[None, :] % HEAD < HEAD // 2, -sine, sine)

    vmem = pl.BlockSpec(memory_space=pltpu.VMEM)
    smem = pl.BlockSpec(memory_space=pltpu.SMEM)
    hbm = pl.BlockSpec(memory_space=pl.ANY)
    dma = pltpu.SemaphoreType.DMA
    V = pltpu.VMEM
    mixed, appended = pl.pallas_call(
        kernel,
        out_shape=(
            jax.ShapeDtypeStruct((STEPS * ROWS, HEAD), f32),
            jax.ShapeDtypeStruct((MEMBERS * STEPS, HEAD), bf16),
        ),
        in_specs=[vmem] * 4 + [smem] * 3 + [hbm] * 5,
        out_specs=(vmem, vmem),
        scratch_shapes=[
            V((STEPS, ROWS, HEAD), bf16), V((1, 2048), f32),
            V((2048, 512), bf16), V((2048, 128), bf16), V((512, 2048), bf16),
            V((SLOTS, PAGE, 1024), bf16), V((SLOTS, PAGE, 1024), bf16),
            V((ROWS, 2048), bf16), V((ROWS, 128), f32), V((GROUPS, 1, 256), f32),
            V((SLOTS, 128), bf16), V((PEERS, SLOTS, 128), bf16), V((256, 128), f32),
            V((256, 256), bf16), V((256, 256), bf16),
            V((16, MEMBERS, HEAD), f32), V((16, MEMBERS, HEAD), f32),
            V((GROUPS, MEMBERS, HEAD), f32), V((GROUPS, MEMBERS, HEAD), f32),
            V((128, 512), bf16),
            V((PEERS, SLOTS, 512), bf16), V((PEERS, SLOTS, 512), bf16),
            V((MEMBERS, HEAD), bf16), V((4, MEMBERS, HEAD), bf16), V((8, MEMBERS, HEAD), bf16),
            V((PEERS, SLOTS, 640), bf16), V((PEERS, SLOTS, 640), bf16),
            V((STEPS, MEMBERS, HEAD), bf16), V((GROUPS, MEMBERS, 512), bf16),
            V((ZN, ROWS, HEAD), f32), V((ZN, ROWS, HEAD), f32), V((ZN, ROWS, HEAD), f32),
            V((ZN, ROWS, HEAD), bf16), V((ZN, ROWS, HEAD), bf16),
            dma((5,)), dma((3,)), dma((4,)), dma, dma, dma((16,)), dma((16,)), dma((4,)),
            dma((4,)), dma, dma((8,)), dma((3,)), dma((4,)), dma((8,)), dma((8,)),
            dma, dma, dma((16,)), dma((16,)), dma((8,)), dma((8,)), dma((8,)),
            dma((8,)), dma((3,)), dma((4,)),
        ],
        compiler_params=pltpu.CompilerParams(
            collective_id=0, has_side_effects=True, vmem_limit_bytes=60 * 1024 * 1024
        ),
        name="paged_attention_layer",
    )(
        x, norm_gain.reshape(16, 128), cosine, sine, lengths, slot_owner, slot_page_number,
        w_query, w_keyval, w_out, paged_key_cache, paged_value_cache,
    )
    return (
        mixed.reshape(ROWS, STEPS, HEAD),
        appended.reshape(MEMBERS, STEPS, HEAD),
    )


def solution(mesh):
    in_specs = (
        P(None, None, "gx"),
        P("gx"),
        P("gx", "gy"),
        P("gx", "gy"),
        P("gy", "gx"),
        P(("gx", "gy", "sa"), None, None),
        P(("gx", "gy", "sa"), None, None),
        P(),
        P(("gx", "gy", "sa")),
        P(("gx", "gy", "sa")),
    )
    out_specs = (P(None, None, ("gx", "gy")), P("gx", None, "gy"))
    return jax.shard_map(local, mesh=mesh, in_specs=in_specs, out_specs=out_specs, check_vma=False)
```
